32 devices in a mesh: grp: 2 (over y), tchunk: 2 (over x), ha: 4 (over z), wa: 2 (over core).
Axes of the slice: x: 2, y: 2, z: 4, core: 2. Of those that a mesh axis runs over, the one named last changes fastest.
Arguments:
- features: bfloat16 [32, 32, 16, 192], P(('grp', 'tchunk'), 'ha', 'wa'), parts along dimension 0, may hold values from -6 to 6
- frame_counts: int32 [4], P(('grp', 'tchunk')), parts along dimension 0, may hold values from 0 to 8, as said below
- gain_first: float32 [192], replicated, may hold values from 0.25 to 1.75
- conv_first: bfloat16 [3, 3, 3, 192, 192], replicated, may hold values from -0.078125 to 0.078125
- bias_first: float32 [192], replicated, may hold values from -1.8 to 1.8
- gain_second: float32 [192], replicated, may hold values from 0.25 to 1.75
- conv_second: bfloat16 [3, 3, 3, 192, 192], replicated, may hold values from -0.078125 to 0.078125
- bias_second: float32 [192], replicated, may hold values from -1.8 to 1.8
Outputs:
- decoded: bfloat16 [32, 32, 16, 192], P(('grp', 'tchunk'), 'ha', 'wa'), parts along dimension 0
The draws below stay inside these ranges and needn't reach their ends.
There are 2 independent parts, one for each index of `grp`. The reference program is written for one: setup_inputs(seed, part) draws one part's arguments, and reference() takes and returns one part's arrays. A program takes and returns all parts, laid end to end along the dimension named above; an argument that names none is the same for every part. Nothing has to cross between parts.
Inputs may be any that keep to these rules, and one draw needn't show every extreme that they name: `frame_counts`: in every draw some temporal block has all 8 slots live; any block may have none.
All inputs are finite; a program needn't handle non-finite values.
Results may differ from the reference program's by a relative error of at most 0.0039.
Values may be sent and summed in bfloat16 or wider, within the bound.
A program may use at most 64 MiB of HBM per device.

```python
import jax
import jax.numpy as jnp
from jax import lax

C = 192
F = 8
FRAMES = 16
HEIGHT = 32
WIDTH = 16
N_TCHUNK = 2


def draw_frame_counts(key, part):
    totals = jax.random.randint(key, (N_TCHUNK,), 0, F + 1)
    chosen = jax.random.randint(jax.random.fold_in(key, 11), (), 0, N_TCHUNK)
    return jnp.where(jnp.arange(N_TCHUNK) == chosen, F, totals).astype(jnp.int32)


def block_scale(rng, extent, shards, low, largest):
    loudness, own = 1.0, jax.random.fold_in(rng, 6)
    for position, blocks in shards:
        heights = jnp.exp(jax.random.uniform(jax.random.fold_in(own, position), (blocks,), jnp.float32, low / len(shards), largest / len(shards)))
        loudness = loudness * jnp.repeat(heights, extent[position] // blocks).reshape([-1 if axis == position else 1 for axis in range(len(extent))])
    return loudness


def bell_draw(key, extent, spread, reach, cuts=(), held_as=jnp.bfloat16):
    values = spread * jax.random.normal(key, extent, jnp.float32)
    if cuts:
        values = values * block_scale(key, extent, cuts, -0.22, 0.18)
    return jnp.clip(values, -reach, reach).astype(held_as)


def setup_inputs(seed: int = 0, part: int = 0) -> dict:
    key_of = jax.random.split(jax.random.key(seed), 9)
    own_keys = jax.random.split(jax.random.fold_in(key_of[8], part), 9)
    return {
        "features": bell_draw(own_keys[0], (FRAMES, HEIGHT, WIDTH, C), 1.0, 6.0, ((0, 2), (1, 4), (2, 2))),
        "frame_counts": draw_frame_counts(jax.random.fold_in(jax.random.fold_in(key_of[8], part), 71), part),
        "gain_first": jnp.clip(1.0 + 0.15 * jax.random.normal(key_of[2], (C,), jnp.float32), 0.25, 1.75),
        "conv_first": bell_draw(key_of[3], (3, 3, 3, C, C), (27 * C) ** -0.5, 0.078125),
        "bias_first": bell_draw(key_of[4], (C,), 0.3, 1.8, (), jnp.float32),
        "gain_second": jnp.clip(1.0 + 0.15 * jax.random.normal(key_of[5], (C,), jnp.float32), 0.25, 1.75),
        "conv_second": bell_draw(key_of[6], (3, 3, 3, C, C), (27 * C) ** -0.5, 0.078125),
        "bias_second": bell_draw(key_of[7], (C,), 0.3, 1.8, (), jnp.float32),
    }


epsilon = 1e-06

def activate(values, gain):
    values = values.astype(jnp.float32)
    inverse = lax.rsqrt(lax.optimization_barrier(jnp.mean(values * values, axis=-1, keepdims=True)) + epsilon)
    return jax.nn.silu(values * inverse * gain).astype(jnp.bfloat16)

def convolve(stacked, kernel, bias_term):
    padded = jnp.pad(stacked.astype(jnp.float32), ((0, 0), (1, 1), (1, 1), (0, 0)))
    result = lax.conv_general_dilated(padded[None], kernel.astype(jnp.float32), (1, 1, 1), 'VALID', dimension_numbers=('NDHWC', 'DHWIO', 'NDHWC'), precision=lax.Precision.HIGHEST)
    return result[0] + bias_term

def reference(features, frame_counts, gain_first, conv_first, bias_first, gain_second, conv_second, bias_second):
    blocks = features.reshape(N_TCHUNK, F, HEIGHT, WIDTH, C)

    def advance(carry, inputs):
        cache_first, cache_second = carry
        block_frames, frame_total = inputs
        valid_mask = (jnp.arange(F) < frame_total)[:, None, None, None]
        first_input = jnp.where(valid_mask, activate(block_frames, gain_first), jnp.zeros_like(block_frames))
        joined_first = jnp.concatenate([cache_first, first_input], axis=0)
        hidden = convolve(joined_first, conv_first, bias_first)
        second_input = jnp.where(valid_mask, activate(hidden, gain_second), jnp.zeros_like(block_frames))
        joined_second = jnp.concatenate([cache_second, second_input], axis=0)
        result = convolve(joined_second, conv_second, bias_second)
        outcome = jnp.where(valid_mask, block_frames.astype(jnp.float32) + result, jnp.zeros((), jnp.float32)).astype(jnp.bfloat16)
        start = frame_total.astype(jnp.int32)
        new_first = lax.dynamic_slice_in_dim(joined_first, start, 2, 0)
        new_second = lax.dynamic_slice_in_dim(joined_second, start, 2, 0)
        return ((new_first, new_second), outcome)
    empty = jnp.zeros((2, HEIGHT, WIDTH, C), jnp.bfloat16)
    final_caches, decoded = lax.scan(advance, (empty, empty), (blocks, frame_counts))
    return decoded.reshape(FRAMES, HEIGHT, WIDTH, C)
```

```python
import functools

import jax
import jax.numpy as jnp
from jax import lax
from jax.experimental import pallas as pl
from jax.experimental.pallas import tpu as pltpu
from jax.sharding import PartitionSpec as P

epsilon = 1e-06
MESH = pl.DeviceIdType.MESH
DIRS = [(dz, dw) for dz in (-1, 0, 1) for dw in (-1, 0, 1)]
f32, bf16 = jnp.float32, jnp.bfloat16


def silu_norm(values, gain):
    inverse = lax.rsqrt(jnp.mean(values * values, axis=-1, keepdims=True) + epsilon)
    return jax.nn.silu(values * inverse * gain)


def both(*conds):
    out = conds[0]
    for c in conds[1:]:
        out = jnp.logical_and(out, c)
    return out


def kernel(sizes, *refs):
    placed, out, scratch = refs[:8], refs[8], refs[9:]
    n_t, n_z, n_w = sizes
    (cnt_ref, feat, g1, w1, b1, g2, w2, b2) = local = scratch[:8]
    frames, rows, cols, chans = feat.shape
    (lsem, even, odd, acc, cnt_own, cnt_in, carry, carry_col, csend, crecv) = scratch[8:18]
    phases = (scratch[18:30], scratch[30:42])
    me_t, me_z, me_w = lax.axis_index("tchunk"), lax.axis_index("ha"), lax.axis_index("wa")
    loads = [pltpu.make_async_copy(src, dst, lsem.at[i]) for i, (src, dst) in enumerate(zip(placed, local))]
    for i in (1, 2, 4, 5, 7, 3, 6):
        loads[i].start()

    def exists(dz, dw):
        z, w = me_z + dz, me_w + dw
        return both(z >= 0, z < n_z, w >= 0, w < n_w)

    def device(k, dz, dw):
        return {"tchunk": k, "ha": lax.rem(me_z + dz + n_z, n_z), "wa": lax.rem(me_w + dw + n_w, n_w)}

    barrier = pltpu.get_barrier_semaphore()
    expected = jnp.int32(0)
    for k in range(n_t):
        for dz, dw in DIRS:
            there = exists(dz, dw)
            if (dz, dw) == (0, 0):
                there = me_t != k
            expected = expected + there.astype(jnp.int32)

            @pl.when(there)
            def _(k=k, dz=dz, dw=dw):
                pl.semaphore_signal(barrier, inc=1, device_id=device(k, dz, dw), device_id_type=MESH)

    x_of = lax.broadcasted_iota(jnp.int32, (frames, cols, chans), 1)
    t_of = lax.broadcasted_iota(jnp.int32, (frames, cols, chans), 0)
    def near(bufs, dz, dw):
        own, own_col, _, _, row_in, col_in = bufs[:6]
        y, yy = (0, rows + 1) if dz < 0 else (rows - 1, 0)
        s, ss = (0, 1) if dw < 0 else (1, 0)
        if dw == 0:
            return own.at[y, pl.ds(2, frames)], row_in.at[1 if dz < 0 else 0]
        if dz == 0:
            return own_col.at[s], col_in.at[ss, pl.ds(1, rows)]
        return own_col.at[s, y], col_in.at[ss, yy]

    def far(bufs, slot, dz, dw):
        tail, tail_col, tail_in, tailc_in = bufs[2], bufs[3], bufs[6], bufs[7]
        s, ss = (0, 1) if dw < 0 else (1, 0)
        if dw == 0:
            if dz == 0:
                return tail, tail_in.at[slot, pl.ds(1, rows)]
            y, yy = (0, rows + 1) if dz < 0 else (rows - 1, 0)
            return tail.at[y], tail_in.at[slot, yy]
        return tail_col.at[s], tailc_in.at[slot, ss, 1 - dz]

    def near_copy(bufs, dz, dw, way=1):
        src, dst = near(bufs, dz, dw)
        i = DIRS.index((dz, dw))
        return pltpu.make_async_remote_copy(
            src, dst, bufs[8].at[i], bufs[9].at[i], device_id=device(me_t, way * dz, way * dw), device_id_type=MESH
        )

    def far_copy(bufs, k, slot, dz, dw, way=1):
        src, dst = far(bufs, slot, dz, dw)
        i = DIRS.index((dz, dw))
        return pltpu.make_async_remote_copy(
            src, dst, bufs[10].at[k, i], bufs[11].at[slot, i],
            device_id=device(k, way * dz, way * dw), device_id_type=MESH,
        )

    def count_copy(k, slot):
        return pltpu.make_async_remote_copy(
            cnt_own, cnt_in.at[slot], csend.at[k], crecv.at[slot],
            device_id=device(k, 0, 0), device_id_type=MESH,
        )

    def clear(bufs):
        bufs[0][:, :2] = jnp.zeros((rows, 2, cols, chans), bf16)
        for dz, dw in DIRS:
            if (dz, dw) == (0, 0):
                continue

            @pl.when(jnp.logical_not(exists(-dz, -dw)))
            def _(dz=dz, dw=dw):
                dst = near(bufs, dz, dw)[1]
                dst[...] = jnp.zeros(dst.shape, dst.dtype)
                for k in range(n_t):
                    dst = far(bufs, k, dz, dw)[1]
                    dst[...] = jnp.zeros(dst.shape, dst.dtype)

    def keep(bufs, y, value):
        own, own_col = bufs[0], bufs[1]
        value = jnp.where(live, value, 0.0)
        own[y, 2:] = value.astype(bf16)
        own_col[0, y] = value[:, 0, :].astype(bf16)
        own_col[1, y] = value[:, cols - 1, :].astype(bf16)

    def keep_tail(bufs):
        own, _, tail, tail_col = bufs[:4]
        for f in range(2):
            frame = own[:, count + f].astype(f32)
            tail[:, f] = frame.astype(bf16)
            tail_col[0, f] = frame[:, 0, :].astype(bf16)
            tail_col[1, f] = frame[:, cols - 1, :].astype(bf16)

    def send(bufs, first):
        for k in range(1, n_t):
            @pl.when(me_t < k)
            def _(k=k):
                if first:
                    count_copy(k, me_t).start()
                for dz, dw in DIRS:
                    @pl.when(exists(dz, dw))
                    def _(dz=dz, dw=dw):
                        far_copy(bufs, k, me_t, dz, dw).start()
        for dz, dw in DIRS:
            if (dz, dw) != (0, 0):
                @pl.when(exists(dz, dw))
                def _(dz=dz, dw=dw):
                    near_copy(bufs, dz, dw).start()

    def receive_near(bufs):
        for dz, dw in DIRS:
            if (dz, dw) != (0, 0):
                @pl.when(exists(-dz, -dw))
                def _(dz=dz, dw=dw):
                    near_copy(bufs, dz, dw, -1).wait_recv()

    def receive_far(bufs, first):
        tail_in, tailc_in = bufs[6], bufs[7]
        carry[...] = jnp.zeros(carry.shape, f32)
        carry_col[...] = jnp.zeros(carry_col.shape, f32)
        for k in range(n_t - 1):
            @pl.when(me_t > k)
            def _(k=k):
                if first:
                    count_copy(k, k).wait_recv()
                for dz, dw in DIRS:
                    @pl.when(exists(-dz, -dw))
                    def _(dz=dz, dw=dw):
                        far_copy(bufs, k, k, dz, dw, -1).wait_recv()
                total = cnt_in[k]
                two, one = total > 1.5, total > 0.5

                def merge(ref, index, late0, late1):
                    early0, early1 = ref[index + (0,)], ref[index + (1,)]
                    ref[index + (0,)] = jnp.where(two, late0, jnp.where(one, early1, early0))
                    ref[index + (1,)] = jnp.where(one, late1, early1)

                for yy in range(rows + 2):
                    merge(carry, (yy,), tail_in[k, yy, 0].astype(f32), tail_in[k, yy, 1].astype(f32))
                for s in range(2):
                    for d in range(3):
                        merge(carry_col, (s, d), tailc_in[k, s, d, 0].astype(f32), tailc_in[k, s, d, 1].astype(f32))

    def finish_sends(bufs, first):
        for k in range(1, n_t):
            @pl.when(me_t < k)
            def _(k=k):
                if first:
                    count_copy(k, me_t).wait_send()
                for dz, dw in DIRS:
                    @pl.when(exists(dz, dw))
                    def _(dz=dz, dw=dw):
                        far_copy(bufs, k, me_t, dz, dw).wait_send()
        for dz, dw in DIRS:
            if (dz, dw) != (0, 0):
                @pl.when(exists(dz, dw))
                def _(dz=dz, dw=dw):
                    near_copy(bufs, dz, dw).wait_send()

    def spread(block, col_left, col_right):
        count_t = block.shape[0]
        flat = block.reshape(count_t * cols, chans)
        xi = lax.broadcasted_iota(jnp.int32, block.shape, 1)
        left = pltpu.roll(flat, 1, 0).reshape(block.shape)
        left = jnp.where(xi == 0, jnp.broadcast_to(col_left[:, None, :], block.shape), left)
        right = pltpu.roll(flat, count_t * cols - 1, 0).reshape(block.shape)
        right = jnp.where(xi == cols - 1, jnp.broadcast_to(col_right[:, None, :], block.shape), right)
        return jnp.concatenate(
            [left.reshape(flat.shape), flat, right.reshape(flat.shape)], axis=1
        )

    def place(bufs, yy, block):
        col_in = bufs[5]
        got = spread(block, col_in[0, yy].astype(f32), col_in[1, yy].astype(f32))
        even[yy, 2 * cols :] = got.astype(bf16)
        odd[yy, cols : 2 * cols] = got[:cols].astype(bf16)
        odd[yy, 2 * cols :] = got[cols : (frames - 1) * cols].astype(bf16)

    def place_carry(yy):
        d, at = (0, rows - 1) if yy == 0 else (2, 0) if yy == rows + 1 else (1, yy - 1)
        left = carry_col[0, d, :, pl.ds(at, 1), :].reshape(2, chans)
        right = carry_col[1, d, :, pl.ds(at, 1), :].reshape(2, chans)
        got = spread(carry[yy], left, right)
        even[yy, : 2 * cols] = got.astype(bf16)
        odd[yy, :cols] = got[cols:].astype(bf16)

    def gather(bufs, first):
        own, row_in = bufs[0], bufs[4]
        receive_near(bufs)

        for y in range(rows):
            place(bufs, y + 1, own[y, 2:].astype(f32))

        place(bufs, 0, row_in[0].astype(f32))
        place(bufs, rows + 1, row_in[1].astype(f32))
        receive_far(bufs, first)
        for yy in range(rows + 2):
            place_carry(yy)

    def conv(weights):
        size = frames * cols
        for a in range(3):
            for i in range(3):
                if a == 1:
                    lhs = odd[pl.ds(i, rows)]
                else:
                    lhs = even[pl.ds(i, rows), pl.ds(a * cols, size)]
                part = jnp.dot(
                    lhs.reshape(rows * size, 3 * chans), weights[a * 3 + i], preferred_element_type=f32
                )
                if a + i == 0:
                    acc[...] = part
                else:
                    acc[...] += part

    one, two = phases
    clear(one)
    clear(two)
    for i in (1, 2):
        loads[i].wait()
    count = placed[0][0]
    live = t_of < count
    cnt_own[...] = jnp.full(cnt_own.shape, count.astype(f32), f32)

    for y in range(rows):
        keep(one, y, silu_norm(feat[:, y].astype(f32), g1[...].reshape(1, 1, chans)))

    keep_tail(one)
    pl.semaphore_wait(barrier, expected)
    send(one, True)
    gather(one, True)
    loads[3].wait()
    conv(w1)
    for i in (4, 5, 7):
        loads[i].wait()

    for y in range(rows):
        at = y * frames * cols
        hidden = acc[pl.ds(at, frames * cols)] + b1[...]
        keep(two, y, silu_norm(hidden.reshape(frames, cols, chans), g2[...].reshape(1, 1, chans)))

    keep_tail(two)
    send(two, False)
    gather(two, False)
    loads[6].wait()
    conv(w2)

    for y in range(rows):
        at = y * frames * cols
        result = (acc[pl.ds(at, frames * cols)] + b2[...]).reshape(frames, cols, chans)
        result = feat[:, y].astype(f32) + result
        out[:, y] = jnp.where(live, result, 0.0).astype(bf16)

    finish_sends(one, True)
    finish_sends(two, False)


def shards(sizes, features, frame_counts, gain_first, conv_first, bias_first, gain_second, conv_second, bias_second):
    frames, rows, cols, chans = features.shape
    n_t = sizes[0]
    dma = pltpu.SemaphoreType.DMA
    phase = [
        pltpu.VMEM((rows, frames + 2, cols, chans), bf16),
        pltpu.VMEM((2, rows, frames, chans), bf16),
        pltpu.VMEM((rows, 2, cols, chans), bf16),
        pltpu.VMEM((2, 2, rows, chans), bf16),
        pltpu.VMEM((2, frames, cols, chans), bf16),
        pltpu.VMEM((2, rows + 2, frames, chans), bf16),
        pltpu.VMEM((n_t, rows + 2, 2, cols, chans), bf16),
        pltpu.VMEM((n_t, 2, 3, 2, rows, chans), bf16),
        dma((len(DIRS),)),
        dma((len(DIRS),)),
        dma((n_t, len(DIRS))),
        dma((n_t, len(DIRS))),
    ]
    scratch = [
        pltpu.SMEM((1,), jnp.int32),
        pltpu.VMEM(features.shape, bf16),
        pltpu.VMEM((1, chans), f32),
        pltpu.VMEM((9, 3 * chans, chans), bf16),
        pltpu.VMEM((1, chans), f32),
        pltpu.VMEM((1, chans), f32),
        pltpu.VMEM((9, 3 * chans, chans), bf16),
        pltpu.VMEM((1, chans), f32),
        dma((8,)),
        pltpu.VMEM((rows + 2, (frames + 2) * cols, 3 * chans), bf16),
        pltpu.VMEM((rows + 2, frames * cols, 3 * chans), bf16),
        pltpu.VMEM((rows * frames * cols, chans), f32),
        pltpu.VMEM((cols, chans), f32),
        pltpu.VMEM((n_t, cols, chans), f32),
        pltpu.VMEM((rows + 2, 2, cols, chans), f32),
        pltpu.VMEM((2, 3, 2, rows, chans), f32),
        dma((n_t,)),
        dma((n_t,)),
    ]
    vmem = pl.BlockSpec(memory_space=pltpu.VMEM)
    return pl.pallas_call(
        functools.partial(kernel, sizes),
        out_shape=jax.ShapeDtypeStruct(features.shape, features.dtype),
        in_specs=[pl.BlockSpec(memory_space=pltpu.SMEM)] + [pl.BlockSpec(memory_space=pltpu.HBM)] * 7,
        out_specs=vmem,
        scratch_shapes=scratch + phase + phase,
        compiler_params=pltpu.CompilerParams(
            collective_id=0, has_side_effects=True, vmem_limit_bytes=60 << 20
        ),
    )(
        frame_counts,
        features,
        gain_first.reshape(1, chans),
        conv_first.reshape(9, 3 * chans, chans),
        bias_first.reshape(1, chans),
        gain_second.reshape(1, chans),
        conv_second.reshape(9, 3 * chans, chans),
        bias_second.reshape(1, chans),
    )


def solution(mesh):
    sizes = (mesh.shape["tchunk"], mesh.shape["ha"], mesh.shape["wa"])
    spec = P(("grp", "tchunk"), "ha", "wa", None)
    return jax.shard_map(
        functools.partial(shards, sizes),
        mesh=mesh,
        in_specs=(spec, P(("grp", "tchunk")), P(), P(), P(), P(), P(), P()),
        out_specs=spec,
        check_vma=False,
    )
```
